32 devices in a mesh: blk: 8 (over z, y), slab: 4 (over x, core).
Axes of the slice: x: 2, y: 2, z: 4, core: 2. Of those that a mesh axis runs over, the one named last changes fastest.
Arguments:
- coulomb: bfloat16 [32, 12, 49152], P(None, None, ('blk', 'slab')), may hold values from -6 to 6
- geminal_left: bfloat16 [16, 12, 49152], P(None, None, ('blk', 'slab')), may hold values from -6 to 6
- geminal_right: bfloat16 [32, 12, 49152], P(None, None, ('blk', 'slab')), may hold values from -6 to 6
Outputs:
- v_direct: float32 [16, 32], P(None, ('blk', 'slab'))
- v_exchange: float32 [16, 32], P(None, ('blk', 'slab'))
The draws below stay inside these ranges and needn't reach their ends.
All inputs are finite; a program needn't handle non-finite values.
Results may differ from the reference program's by a relative error of at most 0.0003.
Values may be sent and summed in bfloat16 or wider, within the bound.
A program may use at most 192 MiB of HBM per device.

```python
import jax
import jax.numpy as jnp
from jax import lax

NAUX = 49152
CB = 12
NI = 16
OCC = 32


def shard_levels(rng, shape, split, low, top_value):
    def one(dim, shards_of):
        heights = jax.random.uniform(jax.random.fold_in(jax.random.fold_in(rng, 6), dim), (shards_of,), jnp.float32, low / len(split), top_value / len(split))
        return jnp.repeat(jnp.exp(heights), shape[dim] // shards_of).reshape((-1,) + (1,) * (len(shape) - dim - 1))

    level = one(*split[0])
    for cut in split[1:]:
        level = level * one(*cut)
    return level


def centred(own_key, shape, scale, most, shards=(), held_as=jnp.bfloat16):
    entries = scale * jax.random.normal(own_key, shape, jnp.float32)
    if shards:
        entries = entries * shard_levels(own_key, shape, shards, -0.22, 0.18)
    return jnp.clip(entries, -most, most).astype(held_as)


def setup_inputs(seed: int = 0) -> dict:
    key_list = jax.random.split(jax.random.key(seed), 4)
    return {
        "coulomb": centred(key_list[0], (OCC, CB, NAUX), 1.0, 6.0, ((2, 32),)),
        "geminal_left": centred(key_list[1], (NI, CB, NAUX), 1.0, 6.0, ((2, 32),)),
        "geminal_right": centred(key_list[2], (OCC, CB, NAUX), 1.0, 6.0, ((2, 32),)),
    }


def reference(coulomb, geminal_left, geminal_right):
    contract = (((1,), (1,)), ((), ()))
    occ_count = coulomb.shape[0]
    slab_count = geminal_left.shape[0]
    j_coul = coulomb.reshape(occ_count * CB, NAUX)
    j_right = geminal_right.reshape(occ_count * CB, NAUX)
    i_coul = coulomb[0:slab_count].reshape(slab_count * CB, NAUX)
    i_left = geminal_left.reshape(slab_count * CB, NAUX)
    tile_c = lax.dot_general(j_coul, i_coul, contract, preferred_element_type=jnp.float32)
    tile_f = lax.dot_general(j_right, i_left, contract, preferred_element_type=jnp.float32)
    tile_c = tile_c.reshape(occ_count, CB, slab_count, CB)
    tile_f = tile_f.reshape(occ_count, CB, slab_count, CB)
    factor = 1.0 / (CB * NAUX)
    direct = jnp.sum(tile_c * tile_f, axis=(1, 3)) * factor
    swapped = jnp.sum(tile_c * jnp.transpose(tile_f, (0, 3, 2, 1)), axis=(1, 3)) * factor
    return jnp.transpose(direct), jnp.transpose(swapped)
```

```python
import functools

import jax
import jax.numpy as jnp
from jax import lax
from jax.experimental import pallas as pl
from jax.experimental.pallas import tpu as pltpu
from jax.sharding import PartitionSpec as P

MESH = pl.DeviceIdType.MESH
LANES = 128
GROUPS = 3


def kernel(
    sizes, pad, coul, left, right, out_d, out_e,
    sl_c, sl_f, x_c, x_f, l_c, l_f, r_c, r_f, part, got1, sum1, got2, sum2, got3, fin_c, fin_f,
    load_sem, send1, recv1, send2, recv2, send3, recv3,
):
    blk_n, slab_n = sizes
    occ, cb, aux = coul.shape
    slab_count = left.shape[0]
    tail = slab_count * cb - LANES
    half = occ // 2
    x_n, y_n, z_n = slab_n // 2, 2, blk_n // 2
    plane = x_n * y_n
    rows1 = half * cb
    rows2 = z_n * cb
    blk, slab = lax.axis_index("blk"), lax.axis_index("slab")
    core, x, y, z = slab % 2, slab // 2, blk % 2, blk // 2

    def device(rc, rx, ry, rz):
        return (
            ((z + rz) % z_n) * y_n + (y + ry) % y_n,
            ((x + rx) % x_n) * 2 + (core + rc) % 2,
        )

    plane_steps = [(m // y_n, m % y_n) for m in range(plane)]

    barrier = pltpu.get_barrier_semaphore()
    partners = [device(1, 0, 0, 0)]
    partners += [device(0, rx, ry, 0) for rx, ry in plane_steps[1:]]
    partners += [device(0, 0, 0, rz) for rz in range(1, z_n)]
    for other in partners:
        pl.semaphore_signal(barrier, inc=1, device_id=other, device_id_type=MESH)

    def load(src, dst, sem):
        copy = pltpu.make_async_copy(src, dst, sem)
        copy.start()
        return copy

    loads = [
        load(coul.at[pl.ds(0, slab_count)], sl_c, load_sem.at[0]),
        load(left, sl_f, load_sem.at[1]),
    ]
    row_loads = []
    for k in range(occ):
        rc, m, rz = 1 - k // half, (k % half) // z_n, k % z_n
        b, s = device(rc, *plane_steps[m], rz)
        j = b * slab_n + s
        row_loads.append(
            (
                load(coul.at[j], x_c.at[k], load_sem.at[2 + 2 * k]),
                load(right.at[j], x_f.at[k], load_sem.at[3 + 2 * k]),
            )
        )

    fin_c[...] = jnp.zeros_like(fin_c)
    fin_f[...] = jnp.zeros_like(fin_f)

    def compact(src, dst, gap):
        for i in range(slab_count):
            lo, hi = i * cb, (i + 1) * cb
            cut = min(max(LANES, lo), hi)
            if cut > lo:
                dst[lo:cut, :] = src[i, 0 : cut - lo, :]
            if hi > cut:
                dst[cut + gap : hi + gap, :] = src[i, cut - lo : cb, :]

    r_c[...] = jnp.zeros_like(r_c)
    r_f[...] = jnp.zeros_like(r_f)
    loads[0].wait()
    compact(sl_c, r_c, 0)
    loads[1].wait()
    compact(sl_f, r_f, LANES - tail)

    contract = (((1,), (1,)), ((), ()))
    is_c = lax.broadcasted_iota(jnp.int32, (cb, LANES), 1) < tail

    def tiles(h):
        for k in range(h * half, (h + 1) * half):
            row_loads[k][0].wait()
            l_c[k * pad : k * pad + cb, :] = x_c[k]
            row_loads[k][1].wait()
            l_f[k * pad : k * pad + cb, :] = x_f[k]
        lhs_c = l_c[h * half * pad : (h + 1) * half * pad, :]
        lhs_f = l_f[h * half * pad : (h + 1) * half * pad, :]
        c = lax.dot_general(lhs_c, r_c[...], contract, preferred_element_type=jnp.float32)
        f = lax.dot_general(lhs_f, r_f[...], contract, preferred_element_type=jnp.float32)
        for k in range(half):
            to = (h * half + k) * cb
            ck, fk = c[k * pad : k * pad + cb], f[k * pad : k * pad + cb]
            part[0, to : to + cb, :] = ck[:, :LANES]
            part[1, to : to + cb, :] = jnp.where(is_c, ck[:, LANES:], fk[:, LANES:])
            part[2, to : to + cb, :] = fk[:, :LANES]

    def send(src, dst, ssem, rsem, to):
        copy = pltpu.make_async_remote_copy(
            src_ref=src, dst_ref=dst, send_sem=ssem, recv_sem=rsem, device_id=to, device_id_type=MESH
        )
        copy.start()
        return copy

    tiles(0)
    pl.semaphore_wait(barrier, len(partners))
    copies1 = [
        send(part.at[g, pl.ds(0, rows1)], got1.at[g], send1.at[g], recv1.at[g], device(1, 0, 0, 0))
        for g in range(GROUPS)
    ]
    tiles(1)

    copies2 = []
    for g in range(GROUPS):
        copies1[g].wait_recv()
        sum1[g] = part[g, rows1 : 2 * rows1, :] + got1[g]
        copies2.append(
            [
                send(
                    sum1.at[g, pl.ds(m * rows2, rows2)], got2.at[g, m - 1],
                    send2.at[g, m - 1], recv2.at[g, m - 1], device(0, *plane_steps[m], 0),
                )
                for m in range(1, plane)
            ]
        )

    copies3 = []
    for g in range(GROUPS):
        for copy in copies2[g]:
            copy.wait_recv()
        total = sum1[g, 0:rows2, :]
        for m in range(1, plane):
            total = total + got2[g, m - 1]
        for rz in range(z_n):
            sum2[g, rz] = total[rz * cb : (rz + 1) * cb]
        copies3.append(
            [
                send(
                    sum2.at[g, rz], got3.at[g, rz - 1],
                    send3.at[g, rz - 1], recv3.at[g, rz - 1], device(0, 0, 0, rz),
                )
                for rz in range(1, z_n)
            ]
        )

    shape = fin_c.shape
    q = lax.broadcasted_iota(jnp.int32, shape, 0)
    lane = lax.broadcasted_iota(jnp.int32, shape, 1)
    first = jnp.zeros(shape, jnp.int32)
    for i in range(1, slab_count):
        first = first + jnp.where(lane >= i * cb, cb, 0)
    real = jnp.logical_and(q < cb, lane < slab_count * cb)
    offset = jnp.where(real, lane - first - q, shape[1])
    grid_i = lax.broadcasted_iota(jnp.int32, (slab_count, shape[1]), 0) * cb
    grid_l = lax.broadcasted_iota(jnp.int32, (slab_count, shape[1]), 1)
    in_i = jnp.logical_and(grid_l >= grid_i, grid_l < grid_i + cb)

    mine = []
    for g in range(GROUPS):
        for copy in copies3[g]:
            copy.wait_recv()
        total = sum2[g, 0]
        for rz in range(1, z_n):
            total = total + got3[g, rz - 1]
        mine.append(total)
    fin_c[0:cb, 0:LANES] = mine[0]
    fin_c[0:cb, LANES:] = mine[1]
    fin_f[0:cb, 0:LANES] = mine[2]
    fin_f[0:cb, LANES:] = pltpu.roll(mine[1], tail, 1)
    c, f = fin_c[...], fin_f[...]
    factor = 1.0 / (cb * aux * blk_n * slab_n)

    def per_i(product):
        row = jnp.sum(product, axis=0, keepdims=True)
        return jnp.sum(jnp.where(in_i, row, 0.0), axis=1, keepdims=True) * factor

    out_d[...] = per_i(jnp.where(real, c * f, 0.0))
    swapped = jnp.zeros(shape, jnp.float32)
    for d in range(1 - cb, cb):
        moved = f
        if d:
            moved = pltpu.roll(pltpu.roll(f, (-d) % shape[0], 0), d % shape[1], 1)
        swapped = jnp.where(offset == d, moved, swapped)
    out_e[...] = per_i(c * swapped)

    for g in range(GROUPS):
        copies1[g].wait_send()
        for copy in copies2[g] + copies3[g]:
            copy.wait_send()


def on_device(sizes, coulomb, geminal_left, geminal_right):
    occ, cb, aux = coulomb.shape
    slab_count = geminal_left.shape[0]
    blk_n, slab_n = sizes
    assert occ == blk_n * slab_n and LANES < slab_count * cb <= 3 * LANES // 2
    half, z_n, plane = occ // 2, blk_n // 2, slab_n
    pad = 16 * -(-cb // 16)
    f32, bf16 = jnp.float32, jnp.bfloat16
    dma = pltpu.SemaphoreType.DMA
    out = jax.ShapeDtypeStruct((slab_count, 1), f32)
    return pl.pallas_call(
        functools.partial(kernel, sizes, pad),
        out_shape=(out, out),
        in_specs=[pl.BlockSpec(memory_space=pl.ANY)] * 3,
        out_specs=(pl.BlockSpec(memory_space=pltpu.VMEM),) * 2,
        scratch_shapes=[
            pltpu.VMEM((slab_count, cb, aux), bf16),
            pltpu.VMEM((slab_count, cb, aux), bf16),
            pltpu.VMEM((occ, cb, aux), bf16),
            pltpu.VMEM((occ, cb, aux), bf16),
            pltpu.VMEM((occ * pad, aux), bf16),
            pltpu.VMEM((occ * pad, aux), bf16),
            pltpu.VMEM((2 * LANES, aux), bf16),
            pltpu.VMEM((2 * LANES, aux), bf16),
            pltpu.VMEM((GROUPS, occ * cb, LANES), f32),
            pltpu.VMEM((GROUPS, half * cb, LANES), f32),
            pltpu.VMEM((GROUPS, half * cb, LANES), f32),
            pltpu.VMEM((GROUPS, plane - 1, z_n * cb, LANES), f32),
            pltpu.VMEM((GROUPS, z_n, cb, LANES), f32),
            pltpu.VMEM((GROUPS, z_n - 1, cb, LANES), f32),
            pltpu.VMEM((pad, 2 * LANES), f32),
            pltpu.VMEM((pad, 2 * LANES), f32),
            dma((2 + 2 * occ,)),
            dma((GROUPS,)),
            dma((GROUPS,)),
            dma((GROUPS, plane - 1)),
            dma((GROUPS, plane - 1)),
            dma((GROUPS, z_n - 1)),
            dma((GROUPS, z_n - 1)),
        ],
        compiler_params=pltpu.CompilerParams(
            collective_id=0, has_side_effects=True, vmem_limit_bytes=48 * 1024 * 1024
        ),
    )(coulomb, geminal_left, geminal_right)


def solution(mesh):
    sizes = (mesh.shape["blk"], mesh.shape["slab"])
    placed = (P(None, None, ("blk", "slab")),) * 3
    return jax.shard_map(
        functools.partial(on_device, sizes),
        mesh=mesh,
        in_specs=placed,
        out_specs=(P(None, ("blk", "slab")), P(None, ("blk", "slab"))),
        check_vma=False,
    )
```

```python
import functools

import jax
import jax.numpy as jnp
from jax import lax
from jax.experimental import pallas as pl
from jax.experimental.pallas import tpu as pltpu
from jax.sharding import PartitionSpec as P

MESH = pl.DeviceIdType.MESH
LANES = 128
GROUPS = 3


def kernel(
    sizes, coul, left, right, out_d, out_e,
    s_c, s_f, x_c, x_f, prod, part, got1, sum1, piece2, got2, sum2, piece3, got3, fin_c, fin_f,
    load_sem, send1, recv1, send2, recv2, send3, recv3,
):
    blk_n, slab_n = sizes
    cb, occ, aux = coul.shape
    slab_count = left.shape[1]
    tail = slab_count * cb - LANES
    x_n, y_n, z_n = slab_n // 2, 2, blk_n // 2
    plane = x_n * y_n
    blk, slab = lax.axis_index("blk"), lax.axis_index("slab")
    core, x, y, z = slab % 2, slab // 2, blk % 2, blk // 2

    def device(rc, rx, ry, rz):
        return (
            ((z + rz) % z_n) * y_n + (y + ry) % y_n,
            ((x + rx) % x_n) * 2 + (core + rc) % 2,
        )

    plane_steps = [(m // y_n, m % y_n) for m in range(plane)]

    def spot(m):
        rx, ry = plane_steps[m]
        return ((y + ry) % y_n) * x_n + (x + rx) % x_n

    barrier = pltpu.get_barrier_semaphore()
    partners = [device(1, 0, 0, 0)]
    partners += [device(0, rx, ry, 0) for rx, ry in plane_steps[1:]]
    partners += [device(0, 0, 0, rz) for rz in range(1, z_n)]
    for other in partners:
        pl.semaphore_signal(barrier, inc=1, device_id=other, device_id_type=MESH)

    def load(src, dst, k):
        copy = pltpu.make_async_copy(src, dst, load_sem.at[k])
        copy.start()
        return copy

    loads = [
        load(coul.at[:, pl.ds(0, slab_count)], s_c, 0),
        load(coul, x_c, 1),
        load(left, s_f, 2),
        load(right, x_f, 3),
    ]
    fin_c[...] = jnp.zeros_like(fin_c)
    fin_f[...] = jnp.zeros_like(fin_f)

    def send(src, dst, ssem, rsem, to):
        copy = pltpu.make_async_remote_copy(
            src_ref=src, dst_ref=dst, send_sem=ssem, recv_sem=rsem, device_id=to, device_id_type=MESH
        )
        copy.start()
        return copy

    contract = (((1,), (1,)), ((), ()))

    def tile(rows, slabs):
        return lax.dot_general(
            rows[...].reshape(cb * occ, aux), slabs[...].reshape(cb * slab_count, aux),
            contract, preferred_element_type=jnp.float32,
        )

    def exchange1(g):
        for parity in range(2):
            part[g, parity] = prod[g, pl.ds(parity, cb * occ // 2, stride=2), :]
        return send(part.at[g, 1 - core], got1.at[g], send1.at[g], recv1.at[g], device(1, 0, 0, 0))

    loads[0].wait()
    loads[1].wait()
    c = tile(x_c, s_c)
    prod[0] = c[:, :LANES]
    prod[1, :, 0:tail] = c[:, LANES:]
    pl.semaphore_wait(barrier, len(partners))
    copies1 = [exchange1(0)]
    loads[2].wait()
    loads[3].wait()
    f = tile(x_f, s_f)
    prod[2] = f[:, :LANES]
    prod[1, :, tail:] = f[:, LANES:]
    copies1.append(exchange1(1))
    copies1.append(exchange1(2))

    copies2 = []
    for g in range(GROUPS):
        copies1[g].wait_recv()
        sum1[g] = part[g, core] + got1[g]
        for m in range(plane):
            piece2[g, m] = sum1[g, pl.ds(m, cb * z_n, stride=plane), :]
        copies2.append(
            [
                send(
                    piece2.at[g, spot(m)], got2.at[g, m - 1],
                    send2.at[g, m - 1], recv2.at[g, m - 1], device(0, *plane_steps[m], 0),
                )
                for m in range(1, plane)
            ]
        )

    copies3 = []
    for g in range(GROUPS):
        for copy in copies2[g]:
            copy.wait_recv()
        total = piece2[g, spot(0)]
        for m in range(1, plane):
            total = total + got2[g, m - 1]
        sum2[g] = total
        for k in range(z_n):
            piece3[g, k] = sum2[g, pl.ds(k, cb, stride=z_n), :]
        copies3.append(
            [
                send(
                    piece3.at[g, (z + rz) % z_n], got3.at[g, rz - 1],
                    send3.at[g, rz - 1], recv3.at[g, rz - 1], device(0, 0, 0, rz),
                )
                for rz in range(1, z_n)
            ]
        )

    shape = fin_c.shape
    q = lax.broadcasted_iota(jnp.int32, shape, 0)
    lane = lax.broadcasted_iota(jnp.int32, shape, 1)
    p = jnp.zeros(shape, jnp.int32)
    for k in range(1, cb):
        p = p + jnp.where(lane >= k * slab_count, 1, 0)
    real = jnp.logical_and(q < cb, lane < slab_count * cb)
    offset = jnp.where(real, p - q, 2 * cb)

    mine = []
    for g in range(GROUPS):
        for copy in copies3[g]:
            copy.wait_recv()
        total = piece3[g, z]
        for rz in range(1, z_n):
            total = total + got3[g, rz - 1]
        mine.append(total)
    fin_c[0:cb, 0:LANES] = mine[0]
    fin_c[0:cb, LANES:] = mine[1]
    fin_f[0:cb, 0:LANES] = mine[2]
    fin_f[0:cb, LANES:] = pltpu.roll(mine[1], LANES - tail, 1)
    c, f = fin_c[...], fin_f[...]
    factor = 1.0 / (cb * aux * blk_n * slab_n)

    def per_i(product):
        row = jnp.sum(product, axis=0, keepdims=True)
        total = row[:, 0:slab_count]
        for k in range(1, cb):
            total = total + row[:, k * slab_count : (k + 1) * slab_count]
        return total * factor

    out_d[...] = per_i(jnp.where(real, c * f, 0.0))
    swapped = jnp.zeros(shape, jnp.float32)
    for d in range(1 - cb, cb):
        moved = f
        if d:
            moved = pltpu.roll(pltpu.roll(f, (-d) % shape[0], 0), d * slab_count % shape[1], 1)
        swapped = jnp.where(offset == d, moved, swapped)
    out_e[...] = per_i(c * swapped)

    for g in range(GROUPS):
        copies1[g].wait_send()
        for copy in copies2[g] + copies3[g]:
            copy.wait_send()


def on_device(sizes, coulomb, geminal_left, geminal_right):
    occ, cb, aux = coulomb.shape
    slab_count = geminal_left.shape[0]
    blk_n, slab_n = sizes
    assert occ == blk_n * slab_n and 2 * slab_count * cb == 3 * LANES
    half, z_n, plane = occ // 2, blk_n // 2, slab_n
    pad = 8 * -(-cb // 8)
    f32, bf16 = jnp.float32, jnp.bfloat16
    dma = pltpu.SemaphoreType.DMA
    out = jax.ShapeDtypeStruct((1, slab_count), f32)
    direct, swapped = pl.pallas_call(
        functools.partial(kernel, sizes),
        out_shape=(out, out),
        in_specs=[pl.BlockSpec(memory_space=pl.ANY)] * 3,
        out_specs=(pl.BlockSpec(memory_space=pltpu.VMEM),) * 2,
        scratch_shapes=[
            pltpu.VMEM((cb, slab_count, aux), bf16),
            pltpu.VMEM((cb, slab_count, aux), bf16),
            pltpu.VMEM((cb, occ, aux), bf16),
            pltpu.VMEM((cb, occ, aux), bf16),
            pltpu.VMEM((GROUPS, cb * occ, LANES), f32),
            pltpu.VMEM((GROUPS, 2, cb * half, LANES), f32),
            pltpu.VMEM((GROUPS, cb * half, LANES), f32),
            pltpu.VMEM((GROUPS, cb * half, LANES), f32),
            pltpu.VMEM((GROUPS, plane, cb * z_n, LANES), f32),
            pltpu.VMEM((GROUPS, plane - 1, cb * z_n, LANES), f32),
            pltpu.VMEM((GROUPS, cb * z_n, LANES), f32),
            pltpu.VMEM((GROUPS, z_n, cb, LANES), f32),
            pltpu.VMEM((GROUPS, z_n - 1, cb, LANES), f32),
            pltpu.VMEM((pad, 2 * LANES), f32),
            pltpu.VMEM((pad, 2 * LANES), f32),
            dma((4,)),
            dma((GROUPS,)),
            dma((GROUPS,)),
            dma((GROUPS, plane - 1)),
            dma((GROUPS, plane - 1)),
            dma((GROUPS, z_n - 1)),
            dma((GROUPS, z_n - 1)),
        ],
        compiler_params=pltpu.CompilerParams(
            collective_id=0, has_side_effects=True, vmem_limit_bytes=67043328
        ),
    )(*(jnp.transpose(a, (1, 0, 2)) for a in (coulomb, geminal_left, geminal_right)))
    return jnp.transpose(direct), jnp.transpose(swapped)


def solution(mesh):
    sizes = (mesh.shape["blk"], mesh.shape["slab"])
    placed = (P(None, None, ("blk", "slab")),) * 3
    return jax.shard_map(
        functools.partial(on_device, sizes),
        mesh=mesh,
        in_specs=placed,
        out_specs=(P(None, ("blk", "slab")), P(None, ("blk", "slab"))),
        check_vma=False,
    )
```

```python
import functools

import jax
import jax.numpy as jnp
from jax import lax
from jax.experimental import pallas as pl
from jax.experimental.pallas import tpu as pltpu
from jax.sharding import PartitionSpec as P

MESH = pl.DeviceIdType.MESH
LANES = 128
GROUPS = 3


def kernel(
    sizes, coul, left, right, out_d, out_e,
    s_c, s_f, x_c, x_f, prod, part, got1, sum1, piece2, got2, sum2, piece3, got3,
    zpiece, zgot, zsum, ppiece, pgot, fin_c, fin_f,
    load_sem, send1, recv1, send2, recv2, send3, recv3, zsend, zrecv, psend, precv,
):
    blk_n, slab_n = sizes
    cb, occ, aux = coul.shape
    slab_count = left.shape[1]
    tail = slab_count * cb - LANES
    x_n, y_n, z_n = slab_n // 2, 2, blk_n // 2
    plane = x_n * y_n
    blk, slab = lax.axis_index("blk"), lax.axis_index("slab")
    core, x, y, z = slab % 2, slab // 2, blk % 2, blk // 2

    def device(rc, rx, ry, rz):
        return (
            ((z + rz) % z_n) * y_n + (y + ry) % y_n,
            ((x + rx) % x_n) * 2 + (core + rc) % 2,
        )

    plane_steps = [(m // y_n, m % y_n) for m in range(plane)]

    def spot(m):
        rx, ry = plane_steps[m]
        return ((y + ry) % y_n) * x_n + (x + rx) % x_n

    barrier = pltpu.get_barrier_semaphore()
    partners = [device(1, 0, 0, 0)]
    partners += [device(0, rx, ry, 0) for rx, ry in plane_steps[1:]]
    partners += [device(0, 0, 0, rz) for rz in range(1, z_n)]
    for other in partners:
        pl.semaphore_signal(barrier, inc=1, device_id=other, device_id_type=MESH)

    def load(src, dst, k):
        copy = pltpu.make_async_copy(src, dst, load_sem.at[k])
        copy.start()
        return copy

    loads = [
        load(coul.at[:, pl.ds(0, slab_count)], s_c, 0),
        load(coul, x_c, 1),
        load(left, s_f, 2),
        load(right, x_f, 3),
    ]
    fin_c[...] = jnp.zeros_like(fin_c)
    fin_f[...] = jnp.zeros_like(fin_f)

    def send(src, dst, ssem, rsem, to):
        copy = pltpu.make_async_remote_copy(
            src_ref=src, dst_ref=dst, send_sem=ssem, recv_sem=rsem, device_id=to, device_id_type=MESH
        )
        copy.start()
        return copy

    contract = (((1,), (1,)), ((), ()))

    def tile(rows, slabs):
        return lax.dot_general(
            rows[...].reshape(cb * occ, aux), slabs[...].reshape(cb * slab_count, aux),
            contract, preferred_element_type=jnp.float32,
        )

    def exchange1(g):
        for parity in range(2):
            part[g, parity] = prod[g, pl.ds(parity, cb * occ // 2, stride=2), :]
        return send(part.at[g, 1 - core], got1.at[g], send1.at[g], recv1.at[g], device(1, 0, 0, 0))

    loads[0].wait()
    loads[1].wait()
    c = tile(x_c, s_c)
    prod[0] = c[:, :LANES]
    prod[1, :, 0:tail] = c[:, LANES:]
    pl.semaphore_wait(barrier, len(partners))
    copies1 = [exchange1(0)]
    loads[2].wait()
    loads[3].wait()
    f = tile(x_f, s_f)
    prod[2] = f[:, :LANES]
    prod[1, :, tail:] = f[:, LANES:]
    copies1.append(exchange1(1))
    copies1.append(exchange1(2))

    copies1[0].wait_recv()
    sum1[0] = part[0, core] + got1[0]
    for k in range(z_n):
        for m in range(plane):
            zpiece[k, pl.ds(m, cb, stride=plane), :] = sum1[
                0, pl.ds(k * plane + m, cb, stride=plane * z_n), :
            ]
    early_z = [
        send(
            zpiece.at[(z + rz) % z_n], zgot.at[rz - 1],
            zsend.at[rz - 1], zrecv.at[rz - 1], device(0, 0, 0, rz),
        )
        for rz in range(1, z_n)
    ]

    copies2 = []
    for g in range(1, GROUPS):
        copies1[g].wait_recv()
        sum1[g] = part[g, core] + got1[g]
        for m in range(plane):
            piece2[g - 1, m] = sum1[g, pl.ds(m, cb * z_n, stride=plane), :]
        copies2.append(
            [
                send(
                    piece2.at[g - 1, spot(m)], got2.at[g - 1, m - 1],
                    send2.at[g - 1, m - 1], recv2.at[g - 1, m - 1], device(0, *plane_steps[m], 0),
                )
                for m in range(1, plane)
            ]
        )

    for copy in early_z:
        copy.wait_recv()
    total = zpiece[z]
    for rz in range(1, z_n):
        total = total + zgot[rz - 1]
    zsum[...] = total
    for m in range(plane):
        ppiece[m] = zsum[pl.ds(m, cb, stride=plane), :]
    late_plane = [
        send(
            ppiece.at[spot(m)], pgot.at[m - 1],
            psend.at[m - 1], precv.at[m - 1], device(0, *plane_steps[m], 0),
        )
        for m in range(1, plane)
    ]

    for g in range(GROUPS - 1):
        for copy in copies2[g]:
            copy.wait_recv()
        total = piece2[g, spot(0)]
        for m in range(1, plane):
            total = total + got2[g, m - 1]
        sum2[g] = total
        for k in range(z_n):
            piece3[k, g * cb : (g + 1) * cb, :] = sum2[g, pl.ds(k, cb, stride=z_n), :]
    copies3 = [
        send(
            piece3.at[(z + rz) % z_n], got3.at[rz - 1],
            send3.at[rz - 1], recv3.at[rz - 1], device(0, 0, 0, rz),
        )
        for rz in range(1, z_n)
    ]

    shape = fin_c.shape
    q = lax.broadcasted_iota(jnp.int32, shape, 0)
    lane = lax.broadcasted_iota(jnp.int32, shape, 1)
    p = jnp.zeros(shape, jnp.int32)
    for k in range(1, cb):
        p = p + jnp.where(lane >= k * slab_count, 1, 0)
    real = jnp.logical_and(q < cb, lane < slab_count * cb)
    offset = jnp.where(real, p - q, 2 * cb)

    for copy in late_plane:
        copy.wait_recv()
    total = ppiece[spot(0)]
    for m in range(1, plane):
        total = total + pgot[m - 1]
    mine = [total]
    for copy in copies3:
        copy.wait_recv()
    total = piece3[z]
    for rz in range(1, z_n):
        total = total + got3[rz - 1]
    mine += [total[:cb], total[cb:]]
    fin_c[0:cb, 0:LANES] = mine[0]
    fin_c[0:cb, LANES:] = mine[1]
    fin_f[0:cb, 0:LANES] = mine[2]
    fin_f[0:cb, LANES:] = pltpu.roll(mine[1], LANES - tail, 1)
    c, f = fin_c[...], fin_f[...]
    factor = 1.0 / (cb * aux * blk_n * slab_n)

    def per_i(product):
        row = jnp.sum(product, axis=0, keepdims=True)
        total = row[:, 0:slab_count]
        for k in range(1, cb):
            total = total + row[:, k * slab_count : (k + 1) * slab_count]
        return total * factor

    out_d[...] = per_i(jnp.where(real, c * f, 0.0))
    swapped = jnp.zeros(shape, jnp.float32)
    for d in range(1 - cb, cb):
        moved = f
        if d:
            moved = pltpu.roll(pltpu.roll(f, (-d) % shape[0], 0), d * slab_count % shape[1], 1)
        swapped = jnp.where(offset == d, moved, swapped)
    out_e[...] = per_i(c * swapped)

    for copy in copies1 + early_z + copies2[0] + copies2[1] + late_plane + copies3:
        copy.wait_send()


def on_device(sizes, coulomb, geminal_left, geminal_right):
    occ, cb, aux = coulomb.shape
    slab_count = geminal_left.shape[0]
    blk_n, slab_n = sizes
    assert occ == blk_n * slab_n and 2 * slab_count * cb == 3 * LANES
    half, z_n, plane = occ // 2, blk_n // 2, slab_n
    pad = 8 * -(-cb // 8)
    f32, bf16 = jnp.float32, jnp.bfloat16
    dma = pltpu.SemaphoreType.DMA
    out = jax.ShapeDtypeStruct((1, slab_count), f32)
    direct, swapped = pl.pallas_call(
        functools.partial(kernel, sizes),
        out_shape=(out, out),
        in_specs=[pl.BlockSpec(memory_space=pl.ANY)] * 3,
        out_specs=(pl.BlockSpec(memory_space=pltpu.VMEM),) * 2,
        scratch_shapes=[
            pltpu.VMEM((cb, slab_count, aux), bf16),
            pltpu.VMEM((cb, slab_count, aux), bf16),
            pltpu.VMEM((cb, occ, aux), bf16),
            pltpu.VMEM((cb, occ, aux), bf16),
            pltpu.VMEM((GROUPS, cb * occ, LANES), f32),
            pltpu.VMEM((GROUPS, 2, cb * half, LANES), f32),
            pltpu.VMEM((GROUPS, cb * half, LANES), f32),
            pltpu.VMEM((GROUPS, cb * half, LANES), f32),
            pltpu.VMEM((GROUPS - 1, plane, cb * z_n, LANES), f32),
            pltpu.VMEM((GROUPS - 1, plane - 1, cb * z_n, LANES), f32),
            pltpu.VMEM((GROUPS - 1, cb * z_n, LANES), f32),
            pltpu.VMEM((z_n, (GROUPS - 1) * cb, LANES), f32),
            pltpu.VMEM((z_n - 1, (GROUPS - 1) * cb, LANES), f32),
            pltpu.VMEM((z_n, cb * plane, LANES), f32),
            pltpu.VMEM((z_n - 1, cb * plane, LANES), f32),
            pltpu.VMEM((cb * plane, LANES), f32),
            pltpu.VMEM((plane, cb, LANES), f32),
            pltpu.VMEM((plane - 1, cb, LANES), f32),
            pltpu.VMEM((pad, 2 * LANES), f32),
            pltpu.VMEM((pad, 2 * LANES), f32),
            dma((4,)),
            dma((GROUPS,)),
            dma((GROUPS,)),
            dma((GROUPS - 1, plane - 1)),
            dma((GROUPS - 1, plane - 1)),
            dma((z_n - 1,)),
            dma((z_n - 1,)),
            dma((z_n - 1,)),
            dma((z_n - 1,)),
            dma((plane - 1,)),
            dma((plane - 1,)),
        ],
        compiler_params=pltpu.CompilerParams(
            collective_id=0, has_side_effects=True, vmem_limit_bytes=67043328
        ),
    )(*(jnp.transpose(a, (1, 0, 2)) for a in (coulomb, geminal_left, geminal_right)))
    return jnp.transpose(direct), jnp.transpose(swapped)


def solution(mesh):
    sizes = (mesh.shape["blk"], mesh.shape["slab"])
    placed = (P(None, None, ("blk", "slab")),) * 3
    return jax.shard_map(
        functools.partial(on_device, sizes),
        mesh=mesh,
        in_specs=placed,
        out_specs=(P(None, ("blk", "slab")), P(None, ("blk", "slab"))),
        check_vma=False,
    )
```

```python
import functools

import jax
import jax.numpy as jnp
from jax import lax
from jax.experimental import pallas as pl
from jax.experimental.pallas import tpu as pltpu
from jax.sharding import PartitionSpec as P

MESH = pl.DeviceIdType.MESH
LANES = 128
GROUPS = 3


def kernel(
    sizes, coul, left, right, out,
    s_f, x_c, x_f, prod, part, got1, sum1, piece2, got2, sum2, piece3, got3,
    zpiece, zgot, zsum, ppiece, pgot,
    load_sem, send1, recv1, send2, recv2, send3, recv3, zsend, zrecv, psend, precv,
):
    blk_n, slab_n = sizes
    cb, occ, aux = coul.shape
    slab_count = left.shape[1]
    tail = slab_count * cb - LANES
    x_n, y_n, z_n = slab_n // 2, 2, blk_n // 2
    plane = x_n * y_n
    blk, slab = lax.axis_index("blk"), lax.axis_index("slab")
    core, x, y, z = slab % 2, slab // 2, blk % 2, blk // 2

    def device(rc, rx, ry, rz):
        return (
            ((z + rz) % z_n) * y_n + (y + ry) % y_n,
            ((x + rx) % x_n) * 2 + (core + rc) % 2,
        )

    plane_steps = [(m // y_n, m % y_n) for m in range(plane)]

    def spot(m):
        rx, ry = plane_steps[m]
        return ((y + ry) % y_n) * x_n + (x + rx) % x_n

    barrier = pltpu.get_barrier_semaphore()
    partners = [device(1, 0, 0, 0)]
    partners += [device(0, rx, ry, 0) for rx, ry in plane_steps[1:]]
    partners += [device(0, 0, 0, rz) for rz in range(1, z_n)]
    for other in partners:
        pl.semaphore_signal(barrier, inc=1, device_id=other, device_id_type=MESH)

    def load(src, dst, k):
        copy = pltpu.make_async_copy(src, dst, load_sem.at[k])
        copy.start()
        return copy

    loads = [
        load(coul, x_c, 0),
        load(left, s_f, 1),
        load(right, x_f, 2),
    ]

    def send(src, dst, ssem, rsem, to):
        copy = pltpu.make_async_remote_copy(
            src_ref=src, dst_ref=dst, send_sem=ssem, recv_sem=rsem, device_id=to, device_id_type=MESH
        )
        copy.start()
        return copy

    contract = (((1,), (1,)), ((), ()))

    def tile(rows, slabs):
        return lax.dot_general(
            rows.reshape(cb * occ, aux), slabs.reshape(cb * slab_count, aux),
            contract, preferred_element_type=jnp.float32,
        )

    def exchange1(g):
        for parity in range(2):
            part[g, parity] = prod[g, pl.ds(parity, cb * occ // 2, stride=2), :]
        return send(part.at[g, 1 - core], got1.at[g], send1.at[g], recv1.at[g], device(1, 0, 0, 0))

    loads[0].wait()
    c = tile(x_c[...], x_c[:, 0:slab_count])
    prod[0] = c[:, :LANES]
    prod[1, :, 0:tail] = c[:, LANES:]
    loads[1].wait()
    loads[2].wait()
    f = tile(x_f[...], s_f[...])
    prod[2] = f[:, :LANES]
    prod[1, :, tail:] = f[:, LANES:]
    pl.semaphore_wait(barrier, len(partners))
    copies1 = [exchange1(g) for g in range(GROUPS)]

    copies1[0].wait_recv()
    sum1[0] = part[0, core] + got1[0]
    for k in range(z_n):
        for m in range(plane):
            zpiece[k, pl.ds(m, cb, stride=plane), :] = sum1[
                0, pl.ds(k * plane + m, cb, stride=plane * z_n), :
            ]
    early_z = [
        send(
            zpiece.at[(z + rz) % z_n], zgot.at[rz - 1],
            zsend.at[rz - 1], zrecv.at[rz - 1], device(0, 0, 0, rz),
        )
        for rz in range(1, z_n)
    ]

    copies2 = []
    for g in range(1, GROUPS):
        copies1[g].wait_recv()
        sum1[g] = part[g, core] + got1[g]
        for m in range(plane):
            piece2[g - 1, m] = sum1[g, pl.ds(m, cb * z_n, stride=plane), :]
        copies2.append(
            [
                send(
                    piece2.at[g - 1, spot(m)], got2.at[g - 1, m - 1],
                    send2.at[g - 1, m - 1], recv2.at[g - 1, m - 1], device(0, *plane_steps[m], 0),
                )
                for m in range(1, plane)
            ]
        )

    for copy in early_z:
        copy.wait_recv()
    total = zpiece[z]
    for rz in range(1, z_n):
        total = total + zgot[rz - 1]
    zsum[...] = total
    for m in range(plane):
        ppiece[m] = zsum[pl.ds(m, cb, stride=plane), :]
    late_plane = [
        send(
            ppiece.at[spot(m)], pgot.at[m - 1],
            psend.at[m - 1], precv.at[m - 1], device(0, *plane_steps[m], 0),
        )
        for m in range(1, plane)
    ]

    for g in range(GROUPS - 1):
        for copy in copies2[g]:
            copy.wait_recv()
        total = piece2[g, spot(0)]
        for m in range(1, plane):
            total = total + got2[g, m - 1]
        sum2[g] = total
        for k in range(z_n):
            piece3[k, g * cb : (g + 1) * cb, :] = sum2[g, pl.ds(k, cb, stride=z_n), :]
    copies3 = [
        send(
            piece3.at[(z + rz) % z_n], got3.at[rz - 1],
            send3.at[rz - 1], recv3.at[rz - 1], device(0, 0, 0, rz),
        )
        for rz in range(1, z_n)
    ]

    for copy in late_plane:
        copy.wait_recv()
    total = ppiece[spot(0)]
    for m in range(1, plane):
        total = total + pgot[m - 1]
    mine = [total]
    for copy in copies3:
        copy.wait_recv()
    total = piece3[z]
    for rz in range(1, z_n):
        total = total + got3[rz - 1]
    mine += [total[:cb], total[cb:]]
    for g in range(GROUPS):
        out[g] = mine[g]
    for copy in copies1 + early_z + copies2[0] + copies2[1] + late_plane + copies3:
        copy.wait_send()


def finish(naux, slab_count, mine, out_d, out_e, fin_c, fin_f):
    cb = mine.shape[1]
    tail = slab_count * cb - LANES
    fin_c[...] = jnp.zeros_like(fin_c)
    fin_f[...] = jnp.zeros_like(fin_f)
    shape = fin_c.shape
    q = lax.broadcasted_iota(jnp.int32, shape, 0)
    lane = lax.broadcasted_iota(jnp.int32, shape, 1)
    p = jnp.zeros(shape, jnp.int32)
    for k in range(1, cb):
        p = p + jnp.where(lane >= k * slab_count, 1, 0)
    real = jnp.logical_and(q < cb, lane < slab_count * cb)
    offset = jnp.where(real, p - q, 2 * cb)

    fin_c[0:cb, 0:LANES] = mine[0]
    fin_c[0:cb, LANES:] = mine[1]
    fin_f[0:cb, 0:LANES] = mine[2]
    fin_f[0:cb, LANES:] = pltpu.roll(mine[1], LANES - tail, 1)
    c, f = fin_c[...], fin_f[...]
    factor = 1.0 / (cb * naux)

    def per_i(product):
        row = jnp.sum(product, axis=0, keepdims=True)
        total = row[:, 0:slab_count]
        for k in range(1, cb):
            total = total + row[:, k * slab_count : (k + 1) * slab_count]
        return total * factor

    out_d[...] = per_i(jnp.where(real, c * f, 0.0))
    swapped = jnp.zeros(shape, jnp.float32)
    for d in range(1 - cb, cb):
        moved = f
        if d:
            moved = pltpu.roll(pltpu.roll(f, (-d) % shape[0], 0), d * slab_count % shape[1], 1)
        swapped = jnp.where(offset == d, moved, swapped)
    out_e[...] = per_i(c * swapped)


def on_device(sizes, coulomb, geminal_left, geminal_right):
    occ, cb, aux = coulomb.shape
    slab_count = geminal_left.shape[0]
    blk_n, slab_n = sizes
    assert occ == blk_n * slab_n and 2 * slab_count * cb == 3 * LANES
    half, z_n, plane = occ // 2, blk_n // 2, slab_n
    pad = 8 * -(-cb // 8)
    f32, bf16 = jnp.float32, jnp.bfloat16
    dma = pltpu.SemaphoreType.DMA
    mine = pl.pallas_call(
        functools.partial(kernel, sizes),
        out_shape=jax.ShapeDtypeStruct((GROUPS, cb, LANES), f32),
        in_specs=[pl.BlockSpec(memory_space=pl.ANY)] * 3,
        out_specs=pl.BlockSpec(memory_space=pltpu.VMEM),
        scratch_shapes=[
            pltpu.VMEM((cb, slab_count, aux), bf16),
            pltpu.VMEM((cb, occ, aux), bf16),
            pltpu.VMEM((cb, occ, aux), bf16),
            pltpu.VMEM((GROUPS, cb * occ, LANES), f32),
            pltpu.VMEM((GROUPS, 2, cb * half, LANES), f32),
            pltpu.VMEM((GROUPS, cb * half, LANES), f32),
            pltpu.VMEM((GROUPS, cb * half, LANES), f32),
            pltpu.VMEM((GROUPS - 1, plane, cb * z_n, LANES), f32),
            pltpu.VMEM((GROUPS - 1, plane - 1, cb * z_n, LANES), f32),
            pltpu.VMEM((GROUPS - 1, cb * z_n, LANES), f32),
            pltpu.VMEM((z_n, (GROUPS - 1) * cb, LANES), f32),
            pltpu.VMEM((z_n - 1, (GROUPS - 1) * cb, LANES), f32),
            pltpu.VMEM((z_n, cb * plane, LANES), f32),
            pltpu.VMEM((z_n - 1, cb * plane, LANES), f32),
            pltpu.VMEM((cb * plane, LANES), f32),
            pltpu.VMEM((plane, cb, LANES), f32),
            pltpu.VMEM((plane - 1, cb, LANES), f32),
            dma((3,)),
            dma((GROUPS,)),
            dma((GROUPS,)),
            dma((GROUPS - 1, plane - 1)),
            dma((GROUPS - 1, plane - 1)),
            dma((z_n - 1,)),
            dma((z_n - 1,)),
            dma((z_n - 1,)),
            dma((z_n - 1,)),
            dma((plane - 1,)),
            dma((plane - 1,)),
        ],
        compiler_params=pltpu.CompilerParams(
            collective_id=0, has_side_effects=True, vmem_limit_bytes=67043328
        ),
    )(*(jnp.transpose(a, (1, 0, 2)) for a in (coulomb, geminal_left, geminal_right)))
    out = jax.ShapeDtypeStruct((1, slab_count), f32)
    direct, swapped = pl.pallas_call(
        functools.partial(finish, aux * blk_n * slab_n, slab_count),
        out_shape=(out, out),
        in_specs=[pl.BlockSpec(memory_space=pltpu.VMEM)],
        out_specs=(pl.BlockSpec(memory_space=pltpu.VMEM),) * 2,
        scratch_shapes=[pltpu.VMEM((pad, 2 * LANES), f32)] * 2,
    )(mine)
    return jnp.transpose(direct), jnp.transpose(swapped)


def solution(mesh):
    sizes = (mesh.shape["blk"], mesh.shape["slab"])
    placed = (P(None, None, ("blk", "slab")),) * 3
    return jax.shard_map(
        functools.partial(on_device, sizes),
        mesh=mesh,
        in_specs=placed,
        out_specs=(P(None, ("blk", "slab")), P(None, ("blk", "slab"))),
        check_vma=False,
    )
```

```python
import functools

import jax
import jax.numpy as jnp
from jax import lax
from jax.experimental import pallas as pl
from jax.experimental.pallas import tpu as pltpu
from jax.sharding import PartitionSpec as P

MESH = pl.DeviceIdType.MESH
LANES = 128
GROUPS = 3


def kernel(
    sizes, coul, left, right, out,
    s_f, x_c, x_f, prod, part, got1, sum1, piece2, got2, sum2, piece3, got3,
    zpiece, zgot, zsum, ppiece, pgot,
    load_sem, send1, recv1, send2, recv2, send3, recv3, zsend, zrecv, psend, precv,
):
    blk_n, slab_n = sizes
    cb, occ, aux = coul.shape
    slab_count = left.shape[1]
    tail = slab_count * cb - LANES
    x_n, y_n, z_n = slab_n // 2, 2, blk_n // 2
    plane = x_n * y_n
    blk, slab = lax.axis_index("blk"), lax.axis_index("slab")
    core, x, y, z = slab % 2, slab // 2, blk % 2, blk // 2

    def device(rc, rx, ry, rz):
        return (
            ((z + rz) % z_n) * y_n + (y + ry) % y_n,
            ((x + rx) % x_n) * 2 + (core + rc) % 2,
        )

    plane_steps = [(m // y_n, m % y_n) for m in range(plane)]

    def spot(m):
        rx, ry = plane_steps[m]
        return ((y + ry) % y_n) * x_n + (x + rx) % x_n

    barrier = pltpu.get_barrier_semaphore()
    partners = [device(1, 0, 0, 0)]
    partners += [device(0, rx, ry, 0) for rx, ry in plane_steps[1:]]
    partners += [device(0, 0, 0, rz) for rz in range(1, z_n)]
    for other in partners:
        pl.semaphore_signal(barrier, inc=1, device_id=other, device_id_type=MESH)

    def load(src, dst, k):
        copy = pltpu.make_async_copy(src, dst, load_sem.at[k])
        copy.start()
        return copy

    loads = [
        load(coul, x_c, 0),
        load(left, s_f, 1),
        load(right, x_f, 2),
    ]

    def send(src, dst, ssem, rsem, to):
        copy = pltpu.make_async_remote_copy(
            src_ref=src, dst_ref=dst, send_sem=ssem, recv_sem=rsem, device_id=to, device_id_type=MESH
        )
        copy.start()
        return copy

    contract = (((1,), (1,)), ((), ()))

    def tile(rows, slabs):
        return lax.dot_general(
            rows.reshape(cb * occ, aux), slabs.reshape(cb * slab_count, aux),
            contract, preferred_element_type=jnp.float32,
        )

    def exchange1(g):
        for parity in range(2):
            part[g, parity] = prod[g, pl.ds(parity, cb * occ // 2, stride=2), :]
        return send(part.at[g, 1 - core], got1.at[g], send1.at[g], recv1.at[g], device(1, 0, 0, 0))

    loads[0].wait()
    c = tile(x_c[...], x_c[:, 0:slab_count])
    prod[0] = c[:, :LANES]
    prod[1, :, 0:tail] = c[:, LANES:]
    loads[1].wait()
    loads[2].wait()
    f = tile(x_f[...], s_f[...])
    prod[2] = f[:, :LANES]
    prod[1, :, tail:] = f[:, LANES:]
    pl.semaphore_wait(barrier, len(partners))
    copies1 = [exchange1(g) for g in range(GROUPS)]

    copies1[0].wait_recv()
    sum1[0] = part[0, core] + got1[0]
    for k in range(z_n):
        for m in range(plane):
            zpiece[k, pl.ds(m, cb, stride=plane), :] = sum1[
                0, pl.ds(k * plane + m, cb, stride=plane * z_n), :
            ]
    early_z = [
        send(
            zpiece.at[(z + rz) % z_n], zgot.at[rz - 1],
            zsend.at[rz - 1], zrecv.at[rz - 1], device(0, 0, 0, rz),
        )
        for rz in range(1, z_n)
    ]

    copies2 = []
    for g in range(1, GROUPS):
        copies1[g].wait_recv()
        sum1[g] = part[g, core] + got1[g]
        for m in range(plane):
            piece2[g - 1, m] = sum1[g, pl.ds(m, cb * z_n, stride=plane), :]
        copies2.append(
            [
                send(
                    piece2.at[g - 1, spot(m)], got2.at[g - 1, m - 1],
                    send2.at[g - 1, m - 1], recv2.at[g - 1, m - 1], device(0, *plane_steps[m], 0),
                )
                for m in range(1, plane)
            ]
        )

    for copy in early_z:
        copy.wait_recv()
    total = zpiece[z]
    for rz in range(1, z_n):
        total = total + zgot[rz - 1]
    zsum[...] = total
    for m in range(plane):
        ppiece[m] = zsum[pl.ds(m, cb, stride=plane), :]
    late_plane = [
        send(
            ppiece.at[spot(m)], pgot.at[m - 1],
            psend.at[m - 1], precv.at[m - 1], device(0, *plane_steps[m], 0),
        )
        for m in range(1, plane)
    ]

    for g in range(GROUPS - 1):
        for copy in copies2[g]:
            copy.wait_recv()
        total = piece2[g, spot(0)]
        for m in range(1, plane):
            total = total + got2[g, m - 1]
        sum2[g] = total
        for k in range(z_n):
            piece3[k, g * cb : (g + 1) * cb, :] = sum2[g, pl.ds(k, cb, stride=z_n), :]
    copies3 = [
        send(
            piece3.at[(z + rz) % z_n], got3.at[rz - 1],
            send3.at[rz - 1], recv3.at[rz - 1], device(0, 0, 0, rz),
        )
        for rz in range(1, z_n)
    ]

    for copy in late_plane:
        copy.wait_recv()
    total = ppiece[spot(0)]
    for m in range(1, plane):
        total = total + pgot[m - 1]
    mine = [total]
    for copy in copies3:
        copy.wait_recv()
    total = piece3[z]
    for rz in range(1, z_n):
        total = total + got3[rz - 1]
    mine += [total[:cb], total[cb:]]
    for g in range(GROUPS):
        out[g] = mine[g]
    for copy in copies1 + early_z + copies2[0] + copies2[1] + late_plane + copies3:
        copy.wait_send()


def finish(naux, slab_count, mine, out_d, out_e, fin_c, fin_f):
    cb = mine.shape[1]
    tail = slab_count * cb - LANES
    fin_c[...] = jnp.zeros_like(fin_c)
    fin_f[...] = jnp.zeros_like(fin_f)
    shape = fin_c.shape
    q = lax.broadcasted_iota(jnp.int32, shape, 0)
    lane = lax.broadcasted_iota(jnp.int32, shape, 1)
    p = jnp.zeros(shape, jnp.int32)
    for k in range(1, cb):
        p = p + jnp.where(lane >= k * slab_count, 1, 0)
    real = jnp.logical_and(q < cb, lane < slab_count * cb)
    offset = jnp.where(real, p - q, 2 * cb)

    fin_c[0:cb, 0:LANES] = mine[0]
    fin_c[0:cb, LANES:] = mine[1]
    fin_f[0:cb, 0:LANES] = mine[2]
    fin_f[0:cb, LANES:] = pltpu.roll(mine[1], LANES - tail, 1)
    c, f = fin_c[...], fin_f[...]
    factor = 1.0 / (cb * naux)

    def per_i(product):
        row = jnp.sum(product, axis=0, keepdims=True)
        total = row[:, 0:slab_count]
        for k in range(1, cb):
            total = total + row[:, k * slab_count : (k + 1) * slab_count]
        return total * factor

    out_d[...] = per_i(jnp.where(real, c * f, 0.0))
    swapped = jnp.zeros(shape, jnp.float32)
    for d in range(1 - cb, cb):
        moved = f
        if d:
            moved = pltpu.roll(pltpu.roll(f, (-d) % shape[0], 0), d * slab_count % shape[1], 1)
        swapped = jnp.where(offset == d, moved, swapped)
    out_e[...] = per_i(c * swapped)


def on_device(sizes, coulomb, geminal_left, geminal_right):
    occ, cb, aux = coulomb.shape
    slab_count = geminal_left.shape[0]
    blk_n, slab_n = sizes
    assert occ == blk_n * slab_n and 2 * slab_count * cb == 3 * LANES
    half, z_n, plane = occ // 2, blk_n // 2, slab_n
    pad = 8 * -(-cb // 8)
    f32, bf16 = jnp.float32, jnp.bfloat16
    dma = pltpu.SemaphoreType.DMA
    mine = pl.pallas_call(
        functools.partial(kernel, sizes),
        out_shape=jax.ShapeDtypeStruct((GROUPS, cb, LANES), f32),
        in_specs=[pl.BlockSpec(memory_space=pl.ANY)] * 3,
        out_specs=pl.BlockSpec(memory_space=pltpu.VMEM),
        scratch_shapes=[
            pltpu.VMEM((cb, slab_count, aux), bf16),
            pltpu.VMEM((cb, occ, aux), bf16),
            pltpu.VMEM((cb, occ, aux), bf16),
            pltpu.VMEM((GROUPS, cb * occ, LANES), f32),
            pltpu.VMEM((GROUPS, 2, cb * half, LANES), f32),
            pltpu.VMEM((GROUPS, cb * half, LANES), f32),
            pltpu.VMEM((GROUPS, cb * half, LANES), f32),
            pltpu.VMEM((GROUPS - 1, plane, cb * z_n, LANES), f32),
            pltpu.VMEM((GROUPS - 1, plane - 1, cb * z_n, LANES), f32),
            pltpu.VMEM((GROUPS - 1, cb * z_n, LANES), f32),
            pltpu.VMEM((z_n, (GROUPS - 1) * cb, LANES), f32),
            pltpu.VMEM((z_n - 1, (GROUPS - 1) * cb, LANES), f32),
            pltpu.VMEM((z_n, cb * plane, LANES), f32),
            pltpu.VMEM((z_n - 1, cb * plane, LANES), f32),
            pltpu.VMEM((cb * plane, LANES), f32),
            pltpu.VMEM((plane, cb, LANES), f32),
            pltpu.VMEM((plane - 1, cb, LANES), f32),
            dma((3,)),
            dma((GROUPS,)),
            dma((GROUPS,)),
            dma((GROUPS - 1, plane - 1)),
            dma((GROUPS - 1, plane - 1)),
            dma((z_n - 1,)),
            dma((z_n - 1,)),
            dma((z_n - 1,)),
            dma((z_n - 1,)),
            dma((plane - 1,)),
            dma((plane - 1,)),
        ],
        compiler_params=pltpu.CompilerParams(
            collective_id=0, has_side_effects=True, vmem_limit_bytes=55000 * 1024
        ),
    )(*(jnp.transpose(a, (1, 0, 2)) for a in (coulomb, geminal_left, geminal_right)))
    out = jax.ShapeDtypeStruct((1, slab_count), f32)
    direct, swapped = pl.pallas_call(
        functools.partial(finish, aux * blk_n * slab_n, slab_count),
        out_shape=(out, out),
        in_specs=[pl.BlockSpec(memory_space=pltpu.VMEM)],
        out_specs=(pl.BlockSpec(memory_space=pltpu.VMEM),) * 2,
        scratch_shapes=[pltpu.VMEM((pad, 2 * LANES), f32)] * 2,
        compiler_params=pltpu.CompilerParams(vmem_limit_bytes=4 * 1024 * 1024),
    )(mine)
    return jnp.transpose(direct), jnp.transpose(swapped)


def solution(mesh):
    sizes = (mesh.shape["blk"], mesh.shape["slab"])
    placed = (P(None, None, ("blk", "slab")),) * 3
    return jax.shard_map(
        functools.partial(on_device, sizes),
        mesh=mesh,
        in_specs=placed,
        out_specs=(P(None, ("blk", "slab")), P(None, ("blk", "slab"))),
        check_vma=False,
    )
```
